32 devices in a mesh: section: 4 (over x, core), shard: 4 (over z), replica: 2 (over y).
Axes of the slice: x: 2, y: 2, z: 4, core: 2. Of those that a mesh axis runs over, the one named last changes fastest.
Arguments:
- normed: bfloat16 [4, 2, 1024, 4096], P('section', None, ('shard', 'replica')), may hold values from -0.125 to 0.125
- key_cotangent: bfloat16 [4, 2, 1024, 512], P('section', None, ('shard', 'replica')), may hold values from -12 to 12
- positions: int32 [2, 1024], P(None, ('shard', 'replica')), may hold values from 0 to 1023, as said below
- key_weight: bfloat16 [4, 4096, 512], P('section', 'shard'), may hold values from -0.09375 to 0.09375
Outputs:
- key_weight_grad: bfloat16 [4, 4096, 512], P('section', 'shard')
- passed_grad: bfloat16 [4, 2, 1024, 4096], P('section', None, ('shard', 'replica'))
The draws below stay inside these ranges and needn't reach their ends.
Inputs may be any that keep to these rules, and one draw needn't show every extreme that they name: `positions`: each token's position within its document of the micro-batch; in every micro-batch a document begins at every multiple of 1024 tokens, and in all but the first micro-batch at further places drawn at random.
All inputs are finite; a program needn't handle non-finite values.
Results may differ from the reference program's by a relative error of at most 0.018.
Values may be sent and summed in bfloat16 or wider, within the bound.
No kernel may reach another device: no remote copies, remote signals or barrier semaphores. Data moves between devices by JAX's collectives and lax.ppermute only.
A program may use at most 64 MiB of HBM per device.

```python
import jax
import jax.numpy as jnp
from jax import lax

DW = 4096
KH = 4
HEAD = 128
MB = 2
KW = 512
DW_PAD = 4096
SECTIONS = 4
TOKENS = 1024
N_SHARD = 4
N_REPLICA = 2


def draw_positions(key, part):
    index = jnp.arange(TOKENS, dtype=jnp.int32)
    first_key = jax.random.fold_in(key, 11)
    extra_key = jax.random.fold_in(key, 23)
    span = min(TOKENS, 1024)
    forced = jax.random.randint(first_key, (MB, 1), 1, span)
    fresh = jax.random.randint(extra_key, (MB, TOKENS), 0, 64) == 0
    later = (jnp.arange(MB, dtype=jnp.int32) > 0)[:, None]
    chosen = jnp.logical_or(fresh, index[None, :] == forced)
    starts = jnp.logical_or(jnp.logical_and(chosen, later), (index % 1024 == 0)[None, :])
    marks = jnp.where(starts, index[None, :], 0)
    return (index[None, :] - lax.cummax(marks, axis=1)).astype(jnp.int32)


def level_of(rng, shape, shards, smallest, largest):
    def one(axis_at, shards_of):
        heights = jax.random.uniform(jax.random.fold_in(jax.random.fold_in(rng, 6), axis_at), (shards_of,), jnp.float32, smallest / len(shards), largest / len(shards))
        return jnp.repeat(jnp.exp(heights), shape[axis_at] // shards_of).reshape((-1,) + (1,) * (len(shape) - axis_at - 1))

    level = one(*shards[0])
    for cut in shards[1:]:
        level = level * one(*cut)
    return level


def bell_draw(rng, extent, deviation, bound, pieces=(), kind=jnp.bfloat16):
    gain = level_of(rng, extent, pieces, -0.22, 0.18) if pieces else 1.0
    values = jax.random.normal(rng, extent, jnp.float32) * deviation * gain
    return jnp.minimum(jnp.maximum(values, -bound), bound).astype(kind)


def setup_inputs(seed: int = 0) -> dict:
    key_list = jax.random.split(jax.random.key(seed), 5)
    return {
        "normed": bell_draw(key_list[0], (SECTIONS, MB, TOKENS, DW), (MB * TOKENS) ** -0.5, 0.125, ((0, 4), (2, 8))),
        "key_cotangent": bell_draw(key_list[1], (SECTIONS, MB, TOKENS, KW), 2.0, 12.0, ((0, 4), (2, 8))),
        "positions": draw_positions(jax.random.fold_in(key_list[4], 71), 0),
        "key_weight": bell_draw(key_list[3], (SECTIONS, DW_PAD, KW), DW ** -0.5, 0.09375, ((0, 4), (1, 4))),
    }


def undo_rotation(cotangent, positions):
    half = HEAD // 2
    index = jnp.arange(half, dtype=jnp.float32)
    freq = jnp.power(jnp.float32(500000.0), -2.0 * index / HEAD)
    angle = positions.astype(jnp.float32)[..., None] * freq
    angle = jnp.concatenate([angle, angle], axis=-1)[:, :, None, :]
    cosine = jnp.cos(angle)
    sine = jnp.sin(angle)
    lead = cotangent.shape[:2]
    grads = cotangent.astype(jnp.float32).reshape(lead + (KH, HEAD))
    swapped = jnp.concatenate([grads[..., half:], -grads[..., :half]], axis=-1)
    result = grads * cosine + swapped * sine
    return result.reshape(lead + (KH * HEAD,)).astype(jnp.bfloat16)


def section_work(items, positions):
    normed, cotangent, weight = items
    key_grad = undo_rotation(cotangent, positions)
    input_grad = jnp.einsum("mtk,dk->mtd", key_grad.astype(jnp.float32),
                            weight[:DW].astype(jnp.float32)).astype(jnp.bfloat16)
    per_dev = TOKENS // (N_SHARD * N_REPLICA)
    blocks_in = normed.reshape(MB, N_SHARD, N_REPLICA, per_dev, DW).astype(jnp.float32)
    blocks_key = key_grad.reshape(MB, N_SHARD, N_REPLICA, per_dev, KH * HEAD).astype(jnp.float32)
    terms = jnp.einsum("mcrtd,mcrtk->crdk", blocks_in, blocks_key).astype(jnp.bfloat16)
    terms = lax.optimization_barrier(terms).astype(jnp.float32)
    shard_sum = jnp.sum(terms, axis=0).astype(jnp.bfloat16)
    shard_sum = lax.optimization_barrier(shard_sum).astype(jnp.float32)
    grad = jnp.sum(shard_sum, axis=0).astype(jnp.bfloat16)
    padding = jnp.zeros((weight.shape[0] - DW, KH * HEAD), jnp.bfloat16)
    return input_grad, jnp.concatenate([grad, padding], axis=0)


def reference(normed, key_cotangent, positions, key_weight):
    input_grad, weight_grad = lax.map(lambda items: section_work(items, positions),
                                      (normed, key_cotangent, key_weight))
    passed = jnp.concatenate([input_grad[1:], jnp.zeros_like(input_grad[:1])], axis=0)
    return weight_grad, passed
```

```python
import functools

import jax
import jax.numpy as jnp
from jax import lax
from jax.experimental import pallas as pl
from jax.experimental.pallas import tpu as pltpu
from jax.sharding import PartitionSpec as P

HEAD = 128
AXES = ("section", "shard", "replica")
BF16 = jnp.bfloat16
F32 = jnp.float32


def shifted(value, axis, steps):
    count = lax.axis_size(axis)
    leading, last = (max(0, -steps), min(count, count - steps))
    return lax.ppermute(value, axis, [(source, source + steps) for source in range(leading, last)])


def undo_rotation(cotangent, positions):
    half = HEAD // 2
    heads = cotangent.shape[-1] // HEAD
    index = jnp.arange(half, dtype=F32)
    freq = jnp.power(F32(500000.0), -2.0 * index / HEAD)
    angle = positions.astype(F32)[..., None] * freq
    angle = jnp.concatenate([angle, angle], axis=-1)[:, :, None, :]
    cosine = jnp.cos(angle)
    sine = jnp.sin(angle)
    lead = cotangent.shape[:2]
    grads = cotangent.astype(F32).reshape(lead + (heads, HEAD))
    swapped = jnp.concatenate([grads[..., half:], -grads[..., :half]], axis=-1)
    result = grads * cosine + swapped * sine
    return result.reshape(lead + (heads * HEAD,)).astype(BF16)


def general_device(normed, key_cotangent, positions, key_weight):
    key_grad = undo_rotation(key_cotangent[0], positions)
    width = normed.shape[3]
    local_rows = key_weight[0]
    partial_cols = jnp.einsum(
        "mtk,dk->mtd",
        lax.all_gather(key_grad, "shard", axis=1, tiled=True),
        local_rows,
        preferred_element_type=F32,
    ).astype(BF16)
    moved = lax.all_to_all(partial_cols, "shard", split_axis=1, concat_axis=2, tiled=True)
    input_grad = moved[:, :, :width][None]
    passed = shifted(input_grad, "section", -1)
    steps_tok = normed.shape[1] * normed.shape[2]
    flat_in = normed[0].reshape(steps_tok, width)
    flat_key = key_grad.reshape(steps_tok, key_grad.shape[-1])
    padding = lax.axis_size("shard") * local_rows.shape[0] - width
    padded = jnp.pad(flat_in, ((0, 0), (0, padding)))
    shard_total = lax.psum_scatter(
        lax.dot_general(
            padded, flat_key, (((0,), (0,)), ((), ())), preferred_element_type=F32
        ).astype(BF16),
        "shard",
        scatter_dimension=0,
        tiled=True,
    )
    total = lax.psum(shard_total, "replica")
    return (total[None], passed)


def call(body, out_shape, ids, *args, flops=0):
    nbytes = sum(a.size * a.dtype.itemsize for a in args)
    spec = pl.BlockSpec(memory_space=pltpu.VMEM)
    return pl.pallas_call(
        body,
        out_shape=out_shape,
        in_specs=[pl.BlockSpec(memory_space=pltpu.SMEM)] + [spec] * len(args),
        out_specs=jax.tree.map(lambda _: spec, out_shape),
        cost_estimate=pl.CostEstimate(flops=flops, bytes_accessed=nbytes, transcendentals=0),
    )(ids, *args)


def rotate_body(ids, freq, pos, cot, out):
    micro, tokens = pos.shape
    lane = lax.broadcasted_iota(jnp.int32, (tokens, HEAD), 1)
    for m in range(micro):
        rows = pl.ds(m * tokens, tokens)
        place = jnp.broadcast_to(pos[pl.ds(m, 1), :].astype(F32), (HEAD, tokens))
        angle = jnp.transpose(place) * freq[...]
        cosine = jnp.cos(angle)
        sine = jnp.sin(angle)
        sine = jnp.where(lane < HEAD // 2, sine, -sine)
        for h in range(cot.shape[1] // HEAD):
            cols = pl.ds(h * HEAD, HEAD)
            grad = cot[rows, cols].astype(F32)
            out[rows, cols] = (
                grad * cosine + pltpu.roll(grad, HEAD // 2, 1) * sine
            ).astype(out.dtype)


def outer(rows, keys):
    return lax.dot_general(rows, keys, (((0,), (0,)), ((), ())), preferred_element_type=F32)


def inner(keys, rows):
    return lax.dot_general(keys, rows, (((1,), (1,)), ((), ())), preferred_element_type=F32)


def term_body(slot, ids, normed, keys, other, other_keys, *rest):
    *sums, out = rest
    half = out.shape[0]
    cols = pl.ds(pl.multiple_of(ids[slot] * half, half), half)
    total = outer(normed[:, cols], keys[...]) + outer(other[...], other_keys[...])
    for part in sums:
        total = total + part[...].astype(F32)
    out[...] = total.astype(out.dtype)


def share_body(ids, keys, *rest):
    *blocks, out = rest
    share = out.shape[1] // len(blocks)
    skip = pl.multiple_of(ids[4] * (blocks[0].shape[0] - share), share)
    for i, block in enumerate(blocks):
        part = inner(keys[...], block[pl.ds(skip, share), :])
        out[:, pl.ds(i * share, share)] = part.astype(out.dtype)


def passed_body(ids, keys, w0, w1, w2m, w2e, w3m, w3e, near, far, out):
    replica, end = ids[4], ids[5]
    share = far.shape[1]
    held = w0.shape[0]
    rows = held + share
    for i, (middle, outside) in enumerate(((w0, w0), (w1, w1), (w2m, w2e), (w3m, w3e))):
        block = middle[...] if middle is outside else jnp.where(end == 1, outside[...], middle[...])
        base = ids[6 + i] * rows
        mine = pl.multiple_of(base + replica * share, share)
        theirs = pl.multiple_of(base + (1 - replica) * held, share)
        out[:, pl.ds(mine, held)] = inner(keys[...], block).astype(out.dtype)
        out[:, pl.ds(theirs, share)] = near[:, pl.ds(i * share, share)] if i < 3 else far[...]


def line_device(normed, key_cotangent, positions, key_weight):
    sections, shards, replicas = (lax.axis_size(a) for a in AXES)
    s, z, y = (lax.axis_index(a) for a in AXES)
    micro, tokens, width = normed.shape[1:]
    count = micro * tokens
    keys_wide = key_cotangent.shape[-1]
    rows = key_weight.shape[1]
    half = rows // replicas
    share = rows // 4
    held = rows - share

    def send(value, move):
        pairs = []
        for a in range(sections):
            for b in range(shards):
                for c in range(replicas):
                    target = move(a, b, c)
                    if target is not None and target[0] >= 0:
                        ta, tb, tc = target
                        pairs.append(((a * shards + b) * replicas + c, (ta * shards + tb) * replicas + tc))
        return lax.ppermute(value, AXES, pairs)

    order = jnp.array([[3, 2, 1, 0], [3, 2, 0, 1], [0, 1, 3, 2], [0, 1, 2, 3]], jnp.int32)[z]
    arrive = jnp.array([[0, 1, 2, 3], [1, 0, 2, 3], [2, 3, 1, 0], [3, 2, 1, 0]], jnp.int32)[z]
    end = jnp.logical_or(z == 0, z == shards - 1).astype(jnp.int32)
    ids = jnp.concatenate([order * replicas + y, jnp.stack([y.astype(jnp.int32), end]), arrive])

    flat = normed.reshape(count, width)
    index = jnp.arange(HEAD // 2, dtype=F32)
    freq = jnp.power(F32(500000.0), -2.0 * index / HEAD)
    freq = jnp.concatenate([freq, freq])[None]
    keys = call(rotate_body, jax.ShapeDtypeStruct((count, keys_wide), BF16), ids, freq, positions,
                key_cotangent.reshape(count, keys_wide))

    piece = lax.dynamic_slice(key_weight[0], (y * share, 0), (held, keys_wide))
    g1 = send(piece, lambda a, b, c: (a - 1, b ^ 1, c))
    g2 = send(piece, lambda a, b, c: (a - 1, 3 - b, c) if b in (1, 2) else None)
    g0 = send(piece, lambda a, b, c: (a - 1, b, c))

    def chunk(k):
        block = order[k] * replicas + (1 - y)
        part = lax.dynamic_slice(flat, (0, block * half), (count, half))
        return send(part, lambda a, b, c: (a, b, 1 - c))

    keys_peer = send(keys, lambda a, b, c: (a, b, 1 - c))
    others = [chunk(k) for k in range(4)]
    keys_next = send(keys, lambda a, b, c: (a - 1, b, c))
    keys_next_peer = send(keys, lambda a, b, c: (a - 1, b, 1 - c))

    def term(k, *sums):
        return call(functools.partial(term_body, k), jax.ShapeDtypeStruct((half, keys_wide), BF16), ids,
                    flat, keys, others[k], keys_peer, *sums, flops=4 * count * half * keys_wide)

    inward = lambda a, b, c: (a, 1, c) if b == 0 else (a, 2, c) if b == 3 else None
    across = lambda a, b, c: (a, 3 - b, c) if b in (1, 2) else None
    outward = lambda a, b, c: (a, 0, c) if b == 1 else (a, 3, c) if b == 2 else None

    t0 = term(0)
    a1 = send(t0, inward)
    g3 = send(g1, across)
    t1 = term(1)
    a2 = send(t1, inward)
    b1 = send(t0 + a1, across)
    g4 = send(g2, outward)
    t2 = term(2)
    d = send(t2, inward)
    b2 = send(t1 + a2, across)
    c1 = send(t2 + b1, outward)
    g5 = send(g3, outward)
    mine = term(3, b2, c1, d)
    theirs = send(mine, lambda a, b, c: (a, b, 1 - c))
    weight_grad = jnp.where(y == 0, jnp.concatenate([mine, theirs]), jnp.concatenate([theirs, mine]))

    share_ids = ids
    slot2 = jnp.where(end == 1, g4, g2)
    slot3 = jnp.where(end == 1, g5, g3)
    near = call(share_body, jax.ShapeDtypeStruct((count, 3 * share), BF16), share_ids,
                keys_next_peer, g0, g1, slot2, flops=6 * count * share * keys_wide)
    near = send(near, lambda a, b, c: (a, b, 1 - c))
    far = call(share_body, jax.ShapeDtypeStruct((count, share), BF16), share_ids,
               keys_next_peer, slot3, flops=2 * count * share * keys_wide)
    far = send(far, lambda a, b, c: (a, b, 1 - c))
    passed = call(passed_body, jax.ShapeDtypeStruct((count, width), BF16), ids,
                  keys_next, g0, g1, g2, g4, g3, g5, near, far, flops=2 * count * width * keys_wide)
    return weight_grad[None], passed.reshape(normed.shape)


def solution(mesh):
    in_specs = (
        P("section", None, ("shard", "replica"), None),
        P("section", None, ("shard", "replica"), None),
        P(None, ("shard", "replica")),
        P("section", "shard", None),
    )
    out_specs = (P("section", "shard", None), P("section", None, ("shard", "replica"), None))

    def body(normed, key_cotangent, positions, key_weight):
        line = (
            mesh.shape["shard"] == 4
            and mesh.shape["replica"] == 2
            and key_weight.shape[1] * 4 == normed.shape[3]
            and key_weight.shape[1] % 512 == 0
        )
        form = line_device if line else general_device
        return form(normed, key_cotangent, positions, key_weight)

    return jax.shard_map(body, mesh=mesh, in_specs=in_specs, out_specs=out_specs, check_vma=False)
```

```python
import functools

import jax
import numpy as np
import jax.numpy as jnp
from jax import lax
from jax.experimental import pallas as pl
from jax.experimental.pallas import tpu as pltpu
from jax.sharding import PartitionSpec as P


HEAD = 128
AXES = ("section", "shard", "replica")
BF16 = jnp.bfloat16
F32 = jnp.float32


def shifted(value, axis, steps):
    count = lax.axis_size(axis)
    leading, last = (max(0, -steps), min(count, count - steps))
    return lax.ppermute(value, axis, [(source, source + steps) for source in range(leading, last)])


def undo_rotation(cotangent, positions):
    half = HEAD // 2
    heads = cotangent.shape[-1] // HEAD
    index = jnp.arange(half, dtype=F32)
    freq = jnp.power(F32(500000.0), -2.0 * index / HEAD)
    angle = positions.astype(F32)[..., None] * freq
    angle = jnp.concatenate([angle, angle], axis=-1)[:, :, None, :]
    cosine = jnp.cos(angle)
    sine = jnp.sin(angle)
    lead = cotangent.shape[:2]
    grads = cotangent.astype(F32).reshape(lead + (heads, HEAD))
    swapped = jnp.concatenate([grads[..., half:], -grads[..., :half]], axis=-1)
    result = grads * cosine + swapped * sine
    return result.reshape(lead + (heads * HEAD,)).astype(BF16)


def general_device(normed, key_cotangent, positions, key_weight):
    key_grad = undo_rotation(key_cotangent[0], positions)
    width = normed.shape[3]
    local_rows = key_weight[0]
    partial_cols = jnp.einsum(
        "mtk,dk->mtd",
        lax.all_gather(key_grad, "shard", axis=1, tiled=True),
        local_rows,
        preferred_element_type=F32,
    ).astype(BF16)
    moved = lax.all_to_all(partial_cols, "shard", split_axis=1, concat_axis=2, tiled=True)
    input_grad = moved[:, :, :width][None]
    passed = shifted(input_grad, "section", -1)
    steps_tok = normed.shape[1] * normed.shape[2]
    flat_in = normed[0].reshape(steps_tok, width)
    flat_key = key_grad.reshape(steps_tok, key_grad.shape[-1])
    padding = lax.axis_size("shard") * local_rows.shape[0] - width
    padded = jnp.pad(flat_in, ((0, 0), (0, padding)))
    shard_total = lax.psum_scatter(
        lax.dot_general(
            padded, flat_key, (((0,), (0,)), ((), ())), preferred_element_type=F32
        ).astype(BF16),
        "shard",
        scatter_dimension=0,
        tiled=True,
    )
    total = lax.psum(shard_total, "replica")
    return (total[None], passed)


VMEM_GRANT = 12 * 2**20


def call(body, out_shape, ids, *args, blocks=None, place=None, aliases=None, scratch=(), grant=VMEM_GRANT, flops=0):
    spec = pl.BlockSpec(memory_space=pltpu.VMEM)
    blocks = blocks or {}
    nbytes = sum(a.size * a.dtype.itemsize for i, a in enumerate(args) if i not in blocks)
    in_specs = [blocks.get(i, spec) for i in range(len(args))]
    whole = place or pl.BlockSpec(out_shape.shape, lambda i, ids: (0,) * len(out_shape.shape))
    in_specs = [
        pl.BlockSpec(a.shape, lambda i, ids, n=len(a.shape): (0,) * n) if s is spec else s
        for a, s in zip(args, in_specs)
    ]
    return pl.pallas_call(
        body,
        out_shape=out_shape,
        grid_spec=pltpu.PrefetchScalarGridSpec(
            num_scalar_prefetch=1, grid=(1,), in_specs=in_specs, out_specs=whole,
            scratch_shapes=scratch,
        ),
        compiler_params=pltpu.CompilerParams(vmem_limit_bytes=grant),
        input_output_aliases=aliases or {},
        cost_estimate=pl.CostEstimate(flops=flops, bytes_accessed=nbytes, transcendentals=0),
    )(ids, *args)


def block_of(flat, half, slot):
    return pl.BlockSpec((flat.shape[0], half), lambda i, ids: (0, ids[slot]))


def rotate_body(ids, freq, pos, cot, out):
    micro, tokens = pos.shape
    lane = lax.broadcasted_iota(jnp.int32, (tokens, HEAD), 1)
    for m in range(micro):
        rows = pl.ds(m * tokens, tokens)
        place = jnp.broadcast_to(pos[pl.ds(m, 1), :].astype(F32), (HEAD, tokens))
        angle = jnp.transpose(place) * freq[...]
        cosine = jnp.cos(angle)
        sine = jnp.sin(angle)
        sine = jnp.where(lane < HEAD // 2, sine, -sine)
        for h in range(cot.shape[1] // HEAD):
            cols = pl.ds(h * HEAD, HEAD)
            grad = cot[rows, cols].astype(F32)
            out[rows, cols] = (
                grad * cosine + pltpu.roll(grad, HEAD // 2, 1) * sine
            ).astype(out.dtype)


def copy_body(ids, *refs):
    *parts, out = refs
    at = 0
    for part in parts:
        out[pl.ds(at, part.shape[0]), :] = part[...]
        at += part.shape[0]


def outer(rows, keys):
    return lax.dot_general(rows, keys, (((0,), (0,)), ((), ())), preferred_element_type=F32)


def inner(keys, rows):
    return lax.dot_general(keys, rows, (((1,), (1,)), ((), ())), preferred_element_type=F32)


def term_body(slot, place, ids, normed, ours, theirs, other, *rest):
    *sums, out, rows, sem = rest
    count, half = rows.shape
    cols = pl.ds(pl.multiple_of(ids[slot] * half, half), half)
    fetch = pltpu.make_async_copy(normed.at[:, cols], rows, sem)
    fetch.start()
    total = outer(other[pl.ds(place * count, count), :], theirs[...])
    fetch.wait()
    total = total + outer(rows[...], ours[...])
    for part in sums:
        total = total + part[...].astype(F32)
    out[...] = total.astype(out.dtype)


def share_body(ids, keys, *rest):
    *blocks, out = rest
    count, half = out.shape[0], blocks[0].shape[0]
    for i, block in enumerate(blocks):
        part = inner(keys[pl.ds(count, count), :], block[...])
        out[:, pl.ds(i * half, half)] = part.astype(out.dtype)


def share_pair_body(ids, keys, w2, w4, w3, w5, out):
    count, half = out.shape[0], w2.shape[0]
    for i, (near, far) in enumerate(((w2, w4), (w3, w5))):
        part = inner(keys[pl.ds(count, count), :], near[...] + far[...])
        out[:, pl.ds(i * half, half)] = part.astype(out.dtype)


def passed_body(ids, keys, w0, w1, w2, w4, w3, w5, near, far, out):
    count, half = out.shape[0], w0.shape[0]
    for i in range(4):
        block = (w0, w1)[i][...] if i < 2 else (w2, w3)[i - 2][...] + (w4, w5)[i - 2][...]
        mine = pl.multiple_of(ids[i] * half, half)
        theirs = pl.multiple_of(ids[4 + i] * half, half)
        out[:, pl.ds(mine, half)] = inner(keys[pl.ds(0, count), :], block).astype(out.dtype)
        out[:, pl.ds(theirs, half)] = (near, far)[i // 2][:, pl.ds(i % 2 * half, half)]


def add_body(ids, a, b, out):
    out[...] = (a[...].astype(F32) + b[...].astype(F32)).astype(out.dtype)


def rows_body(ids, mine, theirs, out):
    half = mine.shape[0]
    out[pl.ds(pl.multiple_of(ids[8] * half, half), half), :] = mine[...]
    out[pl.ds(pl.multiple_of((1 - ids[8]) * half, half), half), :] = theirs[...]


def pair_device(normed, key_cotangent, positions, key_weight):
    sections, shards, replicas = (lax.axis_size(a) for a in AXES)
    _, z, y = (lax.axis_index(a) for a in AXES)
    micro, tokens, width = normed.shape[1:]
    count = micro * tokens
    depth = key_cotangent.shape[-1]
    half = key_weight.shape[1] // replicas
    out = lambda *shape: jax.ShapeDtypeStruct(shape, BF16)

    def send(value, line, back=0, swap=0):
        pairs = []
        for a in range(back, sections):
            for b in range(shards):
                for c in range(replicas):
                    if line(b) is not None:
                        target = ((a - back) * shards + line(b)) * replicas + (c ^ swap)
                        pairs.append(((a * shards + b) * replicas + c, target))
        return lax.ppermute(value, AXES, pairs)

    stay = lambda b: b
    flip = lambda b: b ^ 1
    inward = lambda b: {0: 1, 3: 2}.get(b)
    across = lambda b: {1: 2, 2: 1}.get(b)
    outward = lambda b: {1: 0, 2: 3}.get(b)

    last = jnp.where((z == 0) | (z == shards - 1), 3, 2)
    far = jnp.stack([z, z ^ 1, z ^ (5 - last), z ^ last]).astype(jnp.int32) * replicas
    ids = jnp.concatenate([far + y, far + (1 - y), jnp.stack([y, y]).astype(jnp.int32)])

    flat = normed.reshape(count, width)
    index = np.arange(HEAD // 2, dtype=np.float32)
    freq = np.power(np.float32(500000.0), -2.0 * index / HEAD).astype(np.float32)
    freq = jnp.asarray(np.concatenate([freq, freq])[None])

    pack0 = lax.dynamic_slice(flat, (0, ids[7] * half), (count, half))
    other0 = send(pack0, stay, swap=1)
    ours = call(rotate_body, out(count, depth), ids, freq, positions,
                key_cotangent.reshape(count, depth))
    theirs = send(ours, stay, swap=1)
    piece = lax.dynamic_slice(key_weight[0], (y * half, 0), (half, depth))
    w1 = send(piece, flip, back=1)
    w2 = send(piece, across, back=1)
    w0 = send(piece, stay, back=1)
    pack1 = lax.dynamic_slice(flat, (0, ids[6] * half), (count, half))
    other1 = send(pack1, stay, swap=1)
    pack2 = call(copy_body, out(2 * count, half), ids, flat, flat,
                 blocks={0: block_of(flat, half, 5), 1: block_of(flat, half, 4)})
    other2 = send(pack2, stay, swap=1)

    def term(slot, place, other, *sums):
        return call(functools.partial(term_body, slot, place), out(half, depth), ids,
                    flat, ours, theirs, other, *sums, blocks={0: pl.BlockSpec(memory_space=pltpu.HBM)},
                    scratch=[pltpu.VMEM((count, half), BF16), pltpu.SemaphoreType.DMA],
                    flops=4 * count * half * depth)

    def plus(a, b):
        return call(add_body, out(half, depth), ids, a, b)

    term3 = term(3, 0, other0)
    a1 = send(term3, inward)
    w3 = send(w1, across)
    w4 = send(w2, outward)
    both = call(copy_body, out(2 * count, depth), ids, ours, theirs)
    keys = send(both, stay, back=1)
    term2 = term(2, 0, other1)
    a2 = send(term2, inward)
    b1 = send(plus(term3, a1), across)
    w5 = send(w3, outward)
    b2 = send(plus(term2, a2), across)
    c1 = send(term(1, 0, other2, b1), flip)
    near = call(share_body, out(count, 2 * half), ids, keys, w0, w1,
                flops=4 * count * half * depth)
    near = send(near, stay, swap=1)
    far = call(share_pair_body, out(count, 2 * half), ids, keys, w2, w4, w3, w5,
               flops=4 * count * half * depth)
    far = send(far, stay, swap=1)
    mine = term(0, 1, other2, b2, c1)
    rest = send(mine, stay, swap=1)
    passed = call(passed_body, out(count, width), ids, keys, w0, w1, w2, w4, w3, w5, near, far,
                  flops=8 * count * half * depth)
    weight_grad = call(rows_body, out(replicas * half, depth), ids, mine, rest)
    return weight_grad[None], passed.reshape(normed.shape)


def solution(mesh):
    in_specs = (
        P("section", None, ("shard", "replica"), None),
        P("section", None, ("shard", "replica"), None),
        P(None, ("shard", "replica")),
        P("section", "shard", None),
    )
    out_specs = (P("section", "shard", None), P("section", None, ("shard", "replica"), None))

    def body(normed, key_cotangent, positions, key_weight):
        pairs = (
            mesh.shape["shard"] == 4
            and mesh.shape["replica"] == 2
            and key_weight.shape[1] * 4 == normed.shape[3]
            and key_weight.shape[1] % 1024 == 0
        )
        form = pair_device if pairs else general_device
        return form(normed, key_cotangent, positions, key_weight)

    return jax.shard_map(body, mesh=mesh, in_specs=in_specs, out_specs=out_specs, check_vma=False)
```

```python
import functools

import jax
import numpy as np
import jax.numpy as jnp
from jax import lax
from jax.experimental import pallas as pl
from jax.experimental.pallas import tpu as pltpu
from jax.sharding import PartitionSpec as P


HEAD = 128
PARTS = 2
SHARE = 4
AXES = ("section", "shard", "replica")
BF16 = jnp.bfloat16
F32 = jnp.float32


def shifted(value, axis, steps):
    count = lax.axis_size(axis)
    leading, last = (max(0, -steps), min(count, count - steps))
    return lax.ppermute(value, axis, [(source, source + steps) for source in range(leading, last)])


def undo_rotation(cotangent, positions):
    half = HEAD // 2
    heads = cotangent.shape[-1] // HEAD
    index = jnp.arange(half, dtype=F32)
    freq = jnp.power(F32(500000.0), -2.0 * index / HEAD)
    angle = positions.astype(F32)[..., None] * freq
    angle = jnp.concatenate([angle, angle], axis=-1)[:, :, None, :]
    cosine = jnp.cos(angle)
    sine = jnp.sin(angle)
    lead = cotangent.shape[:2]
    grads = cotangent.astype(F32).reshape(lead + (heads, HEAD))
    swapped = jnp.concatenate([grads[..., half:], -grads[..., :half]], axis=-1)
    result = grads * cosine + swapped * sine
    return result.reshape(lead + (heads * HEAD,)).astype(BF16)


def general_device(normed, key_cotangent, positions, key_weight):
    key_grad = undo_rotation(key_cotangent[0], positions)
    width = normed.shape[3]
    local_rows = key_weight[0]
    partial_cols = jnp.einsum(
        "mtk,dk->mtd",
        lax.all_gather(key_grad, "shard", axis=1, tiled=True),
        local_rows,
        preferred_element_type=F32,
    ).astype(BF16)
    moved = lax.all_to_all(partial_cols, "shard", split_axis=1, concat_axis=2, tiled=True)
    input_grad = moved[:, :, :width][None]
    passed = shifted(input_grad, "section", -1)
    steps_tok = normed.shape[1] * normed.shape[2]
    flat_in = normed[0].reshape(steps_tok, width)
    flat_key = key_grad.reshape(steps_tok, key_grad.shape[-1])
    padding = lax.axis_size("shard") * local_rows.shape[0] - width
    padded = jnp.pad(flat_in, ((0, 0), (0, padding)))
    shard_total = lax.psum_scatter(
        lax.dot_general(
            padded, flat_key, (((0,), (0,)), ((), ())), preferred_element_type=F32
        ).astype(BF16),
        "shard",
        scatter_dimension=0,
        tiled=True,
    )
    total = lax.psum(shard_total, "replica")
    return (total[None], passed)


VMEM_GRANT = 12 * 2**20


def call(body, out_shape, ids, *args, blocks=None, place=None, aliases=None, scratch=(), grant=VMEM_GRANT, flops=0):
    spec = pl.BlockSpec(memory_space=pltpu.VMEM)
    blocks = blocks or {}
    nbytes = sum(a.size * a.dtype.itemsize for i, a in enumerate(args) if i not in blocks)
    in_specs = [blocks.get(i, spec) for i in range(len(args))]
    return kernel_call(body, out_shape, ids, args, in_specs, place, aliases, scratch, grant, flops, nbytes, spec)


def kernel_call(body, out_shape, ids, args, in_specs, place, aliases, scratch, grant, flops, nbytes, spec):
    whole = place or pl.BlockSpec(out_shape.shape, lambda i, ids: (0,) * len(out_shape.shape))
    in_specs = [
        pl.BlockSpec(a.shape, lambda i, ids, n=len(a.shape): (0,) * n) if s is spec else s
        for a, s in zip(args, in_specs)
    ]
    return pl.pallas_call(
        body,
        out_shape=out_shape,
        grid_spec=pltpu.PrefetchScalarGridSpec(
            num_scalar_prefetch=1, grid=(1,), in_specs=in_specs, out_specs=whole,
            scratch_shapes=scratch,
        ),
        compiler_params=pltpu.CompilerParams(vmem_limit_bytes=grant),
        input_output_aliases=aliases or {},
        cost_estimate=pl.CostEstimate(flops=flops, bytes_accessed=nbytes, transcendentals=0),
    )(ids, *args)


def block_of(flat, half, slot):
    return pl.BlockSpec((flat.shape[0], half), lambda i, ids: (0, ids[slot]))


def rotate_body(ids, freq, pos, cot, out):
    micro, tokens = pos.shape
    lane = lax.broadcasted_iota(jnp.int32, (tokens, HEAD), 1)
    for m in range(micro):
        rows = pl.ds(m * tokens, tokens)
        place = jnp.broadcast_to(pos[pl.ds(m, 1), :].astype(F32), (HEAD, tokens))
        angle = jnp.transpose(place) * freq[...]
        cosine = jnp.cos(angle)
        sine = jnp.sin(angle)
        sine = jnp.where(lane < HEAD // 2, sine, -sine)
        for h in range(cot.shape[1] // HEAD):
            cols = pl.ds(h * HEAD, HEAD)
            grad = cot[rows, cols].astype(F32)
            out[rows, cols] = (
                grad * cosine + pltpu.roll(grad, HEAD // 2, 1) * sine
            ).astype(out.dtype)


def copy_body(ids, *refs):
    *parts, out = refs
    at = 0
    for part in parts:
        out[pl.ds(at, part.shape[0]), :] = part[...]
        at += part.shape[0]


def outer(rows, keys):
    return lax.dot_general(rows, keys, (((0,), (0,)), ((), ())), preferred_element_type=F32)


def inner(keys, rows):
    return lax.dot_general(keys, rows, (((1,), (1,)), ((), ())), preferred_element_type=F32)


def term_body(slot, at, place, ids, normed, ours, theirs, other, *rest):
    *sums, out, rows, sem = rest
    count, size = rows.shape
    half = other.shape[1]
    cols = pl.ds(pl.multiple_of(ids[slot] * half + at, size), size)
    fetch = pltpu.make_async_copy(normed.at[:, cols], rows, sem)
    fetch.start()
    total = outer(other[pl.ds(place * count, count), pl.ds(at, size)], theirs[...])
    fetch.wait()
    total = total + outer(rows[...], ours[...])
    for part in sums:
        total = total + part[...].astype(F32)
    out[...] = total.astype(out.dtype)


def own_share(ids, block, share):
    skip = pl.multiple_of(ids[8] * (block.shape[0] - share), HEAD)
    return pl.ds(skip, share)


def share_body(ids, keys, *rest):
    *blocks, out = rest
    count, share = out.shape[0], out.shape[1] // len(blocks)
    for i, block in enumerate(blocks):
        part = inner(keys[pl.ds(count, count), :], block[own_share(ids, block, share), :])
        out[:, pl.ds(i * share, share)] = part.astype(out.dtype)


def share_pair_body(ids, keys, one, two, out):
    count, share = out.shape
    mine = own_share(ids, one, share)
    part = inner(keys[pl.ds(count, count), :], one[mine, :] + two[mine, :])
    out[...] = part.astype(out.dtype)


def passed_body(ids, keys, w0, w1, w2, w4, w3, w5, near, mid, far, out):
    count, held, share = out.shape[0], w0.shape[0], mid.shape[1]
    for i in range(4):
        block = (w0, w1)[i][...] if i < 2 else (w2, w3)[i - 2][...] + (w4, w5)[i - 2][...]
        base = lax.div(ids[i] - ids[8], 2) * (held + share)
        mine = pl.multiple_of(base + ids[8] * share, HEAD)
        theirs = pl.multiple_of(base + (1 - ids[8]) * held, HEAD)
        out[:, pl.ds(mine, held)] = inner(keys[pl.ds(0, count), :], block).astype(out.dtype)
        out[:, pl.ds(theirs, share)] = near[:, pl.ds(i * share, share)] if i < 2 else (mid, far)[i - 2][...]


def add_body(ids, a, b, out):
    out[...] = (a[...].astype(F32) + b[...].astype(F32)).astype(out.dtype)


def rows_body(ids, *refs):
    *parts, out = refs
    count, size = len(parts) // 2, parts[0].shape[0]
    for i, part in enumerate(parts):
        half = ids[8] if i < count else 1 - ids[8]
        at = pl.multiple_of((half * count + i % count) * size, size)
        out[pl.ds(at, size), :] = part[...]


def pair_device(normed, key_cotangent, positions, key_weight):
    sections, shards, replicas = (lax.axis_size(a) for a in AXES)
    _, z, y = (lax.axis_index(a) for a in AXES)
    micro, tokens, width = normed.shape[1:]
    count = micro * tokens
    depth = key_cotangent.shape[-1]
    half = key_weight.shape[1] // replicas
    share = key_weight.shape[1] * SHARE // 8
    out = lambda *shape: jax.ShapeDtypeStruct(shape, BF16)

    def send(value, line, back=0, swap=0, drop=0):
        pairs = []
        for a in range(back, sections - drop):
            for b in range(shards):
                for c in range(replicas):
                    if line(b) is not None:
                        target = ((a - back) * shards + line(b)) * replicas + (c ^ swap)
                        pairs.append(((a * shards + b) * replicas + c, target))
        return lax.ppermute(value, AXES, pairs)

    stay = lambda b: b
    flip = lambda b: b ^ 1
    inward = lambda b: {0: 1, 3: 2}.get(b)
    across = lambda b: {1: 2, 2: 1}.get(b)
    outward = lambda b: {1: 0, 2: 3}.get(b)

    last = jnp.where((z == 0) | (z == shards - 1), 3, 2)
    far = jnp.stack([z, z ^ 1, z ^ (5 - last), z ^ last]).astype(jnp.int32) * replicas
    ids = jnp.concatenate([far + y, far + (1 - y), jnp.stack([y, y]).astype(jnp.int32)])

    flat = normed.reshape(count, width)
    index = np.arange(HEAD // 2, dtype=np.float32)
    freq = np.power(np.float32(500000.0), -2.0 * index / HEAD).astype(np.float32)
    freq = jnp.asarray(np.concatenate([freq, freq])[None])

    pack0 = lax.dynamic_slice(flat, (0, ids[7] * half), (count, half))
    other0 = send(pack0, stay, swap=1)
    ours = call(rotate_body, out(count, depth), ids, freq, positions,
                key_cotangent.reshape(count, depth))
    theirs = send(ours, stay, swap=1)
    piece = lax.dynamic_slice(key_weight[0], (y * share, 0), (replicas * half - share, depth))
    w1 = send(piece, flip, back=1)
    w2 = send(piece, across, back=1)
    w0 = send(piece, stay, back=1)
    pack1 = lax.dynamic_slice(flat, (0, ids[6] * half), (count, half))
    other1 = send(pack1, stay, swap=1)
    pack2 = call(copy_body, out(2 * count, half), ids, flat, flat,
                 blocks={0: block_of(flat, half, 5), 1: block_of(flat, half, 4)})
    other2 = send(pack2, stay, swap=1)

    def term(slot, place, other, *sums, part=0, parts=1, blocks=None):
        size = half // parts
        return call(functools.partial(term_body, slot, part * size, place), out(size, depth), ids,
                    flat, ours, theirs, other, *sums,
                    blocks={0: pl.BlockSpec(memory_space=pltpu.HBM)} | (blocks or {}),
                    scratch=[pltpu.VMEM((count, size), BF16), pltpu.SemaphoreType.DMA],
                    flops=4 * count * size * depth)

    def plus(a, b):
        return call(add_body, out(*a.shape), ids, a, b)

    cut = range(PARTS)
    part_of = lambda i: pl.BlockSpec((half // PARTS, depth), lambda n, ids: (i, 0))
    term3 = term(3, 0, other0)
    a1 = send(term3, inward)
    w3 = send(w1, across, drop=1)
    w4 = send(w2, outward, drop=1)
    both = call(copy_body, out(2 * count, depth), ids, ours, theirs)
    keys = send(both, stay, back=1)
    term2 = term(2, 0, other1)
    a2 = send(term2, inward)
    b1 = send(plus(term3, a1), across)
    w5 = send(w3, outward, drop=1)
    b2 = send(plus(term2, a2), across)
    term1 = [term(1, 0, other2, b1, part=i, parts=PARTS, blocks={4: part_of(i)}) for i in cut]
    c1 = [send(term1[i], flip) for i in cut]
    near = call(share_body, out(count, 2 * share), ids, keys, w0, w1,
                flops=4 * count * share * depth)
    near = send(near, stay, swap=1)
    mid = call(share_pair_body, out(count, share), ids, keys, w2, w4, flops=2 * count * share * depth)
    mid = send(mid, stay, swap=1)
    far = call(share_pair_body, out(count, share), ids, keys, w3, w5, flops=2 * count * share * depth)
    far = send(far, stay, swap=1)
    mine = [
        term(0, 1, other2, c1[i], b2, part=i, parts=PARTS,
             blocks={5: part_of(i)})
        for i in cut
    ]
    rest = [send(mine[i], stay, swap=1) for i in cut]
    passed = call(passed_body, out(count, width), ids, keys, w0, w1, w2, w4, w3, w5, near, mid, far,
                  flops=2 * count * width * depth)
    weight_grad = call(rows_body, out(replicas * half, depth), ids, *mine, *rest)
    return weight_grad[None], passed.reshape(normed.shape)


def solution(mesh):
    in_specs = (
        P("section", None, ("shard", "replica"), None),
        P("section", None, ("shard", "replica"), None),
        P(None, ("shard", "replica")),
        P("section", "shard", None),
    )
    out_specs = (P("section", "shard", None), P("section", None, ("shard", "replica"), None))

    def body(normed, key_cotangent, positions, key_weight):
        pairs = (
            mesh.shape["shard"] == 4
            and mesh.shape["replica"] == 2
            and key_weight.shape[1] * 4 == normed.shape[3]
            and key_weight.shape[1] % 1024 == 0
        )
        form = pair_device if pairs else general_device
        return form(normed, key_cotangent, positions, key_weight)

    return jax.shard_map(body, mesh=mesh, in_specs=in_specs, out_specs=out_specs, check_vma=False)
```

```python
import functools
import math

import jax
import jax.numpy as jnp
from jax import lax
from jax.experimental import pallas as pl
from jax.experimental.pallas import tpu as pltpu
from jax.sharding import PartitionSpec as P


HEAD = 128
PARTS = 2
SHARE = 4
AXES = ("section", "shard", "replica")
BF16 = jnp.bfloat16
F32 = jnp.float32


def shifted(value, axis, steps):
    count = lax.axis_size(axis)
    leading, last = (max(0, -steps), min(count, count - steps))
    return lax.ppermute(value, axis, [(source, source + steps) for source in range(leading, last)])


def undo_rotation(cotangent, positions):
    half = HEAD // 2
    heads = cotangent.shape[-1] // HEAD
    index = jnp.arange(half, dtype=F32)
    freq = jnp.power(F32(500000.0), -2.0 * index / HEAD)
    angle = positions.astype(F32)[..., None] * freq
    angle = jnp.concatenate([angle, angle], axis=-1)[:, :, None, :]
    cosine = jnp.cos(angle)
    sine = jnp.sin(angle)
    lead = cotangent.shape[:2]
    grads = cotangent.astype(F32).reshape(lead + (heads, HEAD))
    swapped = jnp.concatenate([grads[..., half:], -grads[..., :half]], axis=-1)
    result = grads * cosine + swapped * sine
    return result.reshape(lead + (heads * HEAD,)).astype(BF16)


def general_device(normed, key_cotangent, positions, key_weight):
    key_grad = undo_rotation(key_cotangent[0], positions)
    width = normed.shape[3]
    local_rows = key_weight[0]
    partial_cols = jnp.einsum(
        "mtk,dk->mtd",
        lax.all_gather(key_grad, "shard", axis=1, tiled=True),
        local_rows,
        preferred_element_type=F32,
    ).astype(BF16)
    moved = lax.all_to_all(partial_cols, "shard", split_axis=1, concat_axis=2, tiled=True)
    input_grad = moved[:, :, :width][None]
    passed = shifted(input_grad, "section", -1)
    steps_tok = normed.shape[1] * normed.shape[2]
    flat_in = normed[0].reshape(steps_tok, width)
    flat_key = key_grad.reshape(steps_tok, key_grad.shape[-1])
    padding = lax.axis_size("shard") * local_rows.shape[0] - width
    padded = jnp.pad(flat_in, ((0, 0), (0, padding)))
    shard_total = lax.psum_scatter(
        lax.dot_general(
            padded, flat_key, (((0,), (0,)), ((), ())), preferred_element_type=F32
        ).astype(BF16),
        "shard",
        scatter_dimension=0,
        tiled=True,
    )
    total = lax.psum(shard_total, "replica")
    return (total[None], passed)


VMEM_GRANT = 12 * 2**20


def call(body, out_shape, ids, *args, blocks=None, place=None, aliases=None, scratch=(), grant=VMEM_GRANT, flops=0):
    spec = pl.BlockSpec(memory_space=pltpu.VMEM)
    blocks = blocks or {}
    nbytes = sum(a.size * a.dtype.itemsize for i, a in enumerate(args) if i not in blocks)
    in_specs = [blocks.get(i, spec) for i in range(len(args))]
    return kernel_call(body, out_shape, ids, args, in_specs, place, aliases, scratch, grant, flops, nbytes, spec)


def kernel_call(body, out_shape, ids, args, in_specs, place, aliases, scratch, grant, flops, nbytes, spec):
    whole = place or pl.BlockSpec(out_shape.shape, lambda i, ids: (0,) * len(out_shape.shape))
    in_specs = [
        pl.BlockSpec(a.shape, lambda i, ids, n=len(a.shape): (0,) * n) if s is spec else s
        for a, s in zip(args, in_specs)
    ]
    return pl.pallas_call(
        body,
        out_shape=out_shape,
        grid_spec=pltpu.PrefetchScalarGridSpec(
            num_scalar_prefetch=1, grid=(1,), in_specs=in_specs, out_specs=whole,
            scratch_shapes=scratch,
        ),
        compiler_params=pltpu.CompilerParams(vmem_limit_bytes=grant),
        input_output_aliases=aliases or {},
        cost_estimate=pl.CostEstimate(flops=flops, bytes_accessed=nbytes, transcendentals=0),
    )(ids, *args)


def block_of(flat, half, slot):
    return pl.BlockSpec((flat.shape[0], half), lambda i, ids: (0, ids[slot]))


def rotate_body(ids, pos, cot, out):
    micro, tokens = pos.shape
    lane = lax.broadcasted_iota(jnp.int32, (tokens, HEAD), 1)
    freq = jnp.exp(lax.rem(lane, HEAD // 2).astype(F32) * (-2.0 / HEAD * math.log(500000.0)))
    for m in range(micro):
        rows = pl.ds(m * tokens, tokens)
        place = jnp.broadcast_to(pos[pl.ds(m, 1), :].astype(F32), (HEAD, tokens))
        angle = jnp.transpose(place) * freq
        cosine = jnp.cos(angle)
        sine = jnp.sin(angle)
        sine = jnp.where(lane < HEAD // 2, sine, -sine)
        for h in range(cot.shape[1] // HEAD):
            cols = pl.ds(h * HEAD, HEAD)
            grad = cot[rows, cols].astype(F32)
            out[rows, cols] = (
                grad * cosine + pltpu.roll(grad, HEAD // 2, 1) * sine
            ).astype(out.dtype)


def copy_body(ids, *refs):
    *parts, out = refs
    at = 0
    for part in parts:
        out[pl.ds(at, part.shape[0]), :] = part[...]
        at += part.shape[0]


def outer(rows, keys):
    return lax.dot_general(rows, keys, (((0,), (0,)), ((), ())), preferred_element_type=F32)


def inner(keys, rows):
    return lax.dot_general(keys, rows, (((1,), (1,)), ((), ())), preferred_element_type=F32)


def term_body(slot, part, place, ids, normed, ours, theirs, other, *rest):
    *sums, out, rows, keys, keys_other, rows_other, held, sems = rest
    count, size = rows.shape
    at = part * size
    cols = pl.ds(pl.multiple_of(ids[slot] * other.shape[1] + at, size), size)
    moves = [
        (other.at[pl.ds(place * count, count), pl.ds(at, size)], rows_other),
        (theirs, keys_other),
        (normed.at[:, cols], rows),
        (ours, keys),
    ]
    for i, add in enumerate(sums):
        moves.append((add.at[pl.ds(at if add.shape[0] > size else 0, size), :], held.at[i]))
    copies = [pltpu.make_async_copy(a, b, sems.at[i]) for i, (a, b) in enumerate(moves)]
    for copy in copies:
        copy.start()
    copies[0].wait()
    copies[1].wait()
    total = outer(rows_other[...], keys_other[...])
    copies[2].wait()
    copies[3].wait()
    total = total + outer(rows[...], keys[...])
    for i in range(len(sums)):
        copies[4 + i].wait()
        total = total + held[i].astype(F32)
    out[...] = total.astype(out.dtype)


def own_share(ids, block, share):
    skip = pl.multiple_of(ids[8] * (block.shape[0] - share), HEAD)
    return pl.ds(skip, share)


def share_body(ids, keys, *rest):
    *blocks, out = rest
    count, share = out.shape[0], out.shape[1] // len(blocks)
    for i, block in enumerate(blocks):
        part = inner(keys[pl.ds(count, count), :], block[own_share(ids, block, share), :])
        out[:, pl.ds(i * share, share)] = part.astype(out.dtype)


def share_pair_body(ids, keys, one, two, out):
    count, share = out.shape
    mine = own_share(ids, one, share)
    part = inner(keys[pl.ds(count, count), :], one[mine, :] + two[mine, :])
    out[...] = part.astype(out.dtype)


def passed_body(ids, keys, w0, w1, w2, w4, w3, w5, near, mid, far, out):
    count, held, share = out.shape[0], w0.shape[0], mid.shape[1]
    for i in range(4):
        block = (w0, w1)[i][...] if i < 2 else (w2, w3)[i - 2][...] + (w4, w5)[i - 2][...]
        base = lax.div(ids[i] - ids[8], 2) * (held + share)
        mine = pl.multiple_of(base + ids[8] * share, HEAD)
        theirs = pl.multiple_of(base + (1 - ids[8]) * held, HEAD)
        out[:, pl.ds(mine, held)] = inner(keys[pl.ds(0, count), :], block).astype(out.dtype)
        out[:, pl.ds(theirs, share)] = near[:, pl.ds(i * share, share)] if i < 2 else (mid, far)[i - 2][...]


def add_body(ids, a, b, out):
    out[...] = (a[...].astype(F32) + b[...].astype(F32)).astype(out.dtype)


def last_body(ids, part, held, out):
    out[...] = part[...]


def rows_body(ids, *refs):
    *parts, out = refs
    count, size = PARTS, parts[0].shape[0]
    for i, part in enumerate(parts):
        half = ids[8] if i < count else 1 - ids[8]
        at = pl.multiple_of((half * count + i % count) * size, size)
        out[pl.ds(at, size), :] = part[...]


def pair_device(normed, key_cotangent, positions, key_weight):
    sections, shards, replicas = (lax.axis_size(a) for a in AXES)
    _, z, y = (lax.axis_index(a) for a in AXES)
    micro, tokens, width = normed.shape[1:]
    count = micro * tokens
    depth = key_cotangent.shape[-1]
    half = key_weight.shape[1] // replicas
    share = key_weight.shape[1] * SHARE // 8
    out = lambda *shape: jax.ShapeDtypeStruct(shape, BF16)

    def send(value, line, back=0, swap=0, drop=0):
        pairs = []
        for a in range(back, sections - drop):
            for b in range(shards):
                for c in range(replicas):
                    if line(b) is not None:
                        target = ((a - back) * shards + line(b)) * replicas + (c ^ swap)
                        pairs.append(((a * shards + b) * replicas + c, target))
        return lax.ppermute(value, AXES, pairs)

    stay = lambda b: b
    flip = lambda b: b ^ 1
    inward = lambda b: {0: 1, 3: 2}.get(b)
    across = lambda b: {1: 2, 2: 1}.get(b)
    outward = lambda b: {1: 0, 2: 3}.get(b)

    last = jnp.where((z == 0) | (z == shards - 1), 3, 2)
    line = [b * replicas for b in (z, z ^ 1, z ^ (5 - last), z ^ last)]
    far = jnp.stack(line).astype(jnp.int32)
    ids = jnp.concatenate([far + y, far + (1 - y), jnp.stack([y, y]).astype(jnp.int32)])

    flat = normed.reshape(count, width)
    pack0 = lax.dynamic_slice(flat, (0, (line[3] + 1 - y) * half), (count, half))
    other0 = send(pack0, stay, swap=1)
    ours = call(rotate_body, out(count, depth), ids, positions,
                key_cotangent.reshape(count, depth))
    theirs = send(ours, stay, swap=1)
    piece = call(copy_body, out(half, depth), ids, key_weight[0],
                 blocks={0: pl.BlockSpec((half, depth), lambda i, ids: (ids[8], 0))})
    w1 = send(piece, flip, back=1)
    w2 = send(piece, across, back=1)
    w0 = send(piece, stay, back=1)
    pack1 = lax.dynamic_slice(flat, (0, (line[2] + 1 - y) * half), (count, half))
    other1 = send(pack1, stay, swap=1)
    pack2 = call(copy_body, out(2 * count, half), ids, flat, flat,
                 blocks={0: block_of(flat, half, 5), 1: block_of(flat, half, 4)})
    other2 = send(pack2, stay, swap=1)

    def term(slot, place, other, *sums, part=0, parts=1):
        size = half // parts
        args = (flat, ours, theirs, other, *sums)
        buffers = [(count, size), (count, depth), (count, depth), (count, size), (max(len(sums), 1), size, depth)]
        return call(functools.partial(term_body, slot, part, place), out(size, depth), ids, *args,
                    blocks={i: pl.BlockSpec(memory_space=pltpu.HBM if i == 0 else pl.ANY) for i in range(len(args))},
                    scratch=[pltpu.VMEM(shape, BF16) for shape in buffers] + [pltpu.SemaphoreType.DMA((len(args),))],
                    flops=4 * count * size * depth)

    def plus(a, b):
        return call(add_body, out(*a.shape), ids, a, b)

    cut = range(PARTS)
    term3 = term(3, 0, other0)
    a1 = send(term3, inward)
    w3 = send(w1, across, drop=1)
    w4 = send(w2, outward, drop=1)
    both = call(copy_body, out(2 * count, depth), ids, ours, theirs)
    keys = send(both, stay, back=1)
    term2 = term(2, 0, other1)
    a2 = send(term2, inward)
    b1 = send(plus(term3, a1), across)
    w5 = send(w3, outward, drop=1)
    b2 = send(plus(term2, a2), across)
    term1 = [term(1, 0, other2, b1, part=i, parts=PARTS) for i in cut]
    c1 = [send(term1[i], flip) for i in cut]
    near = call(share_body, out(count, 2 * share), ids, keys, w0, w1,
                flops=4 * count * share * depth)
    near = send(near, stay, swap=1)
    mid = call(share_pair_body, out(count, share), ids, keys, w2, w4, flops=2 * count * share * depth)
    mid = send(mid, stay, swap=1)
    far = call(share_pair_body, out(count, share), ids, keys, w3, w5, flops=2 * count * share * depth)
    far = send(far, stay, swap=1)
    mine = [term(0, 1, other2, c1[i], b2, part=i, parts=PARTS) for i in cut]
    rest = [send(mine[i], stay, swap=1) for i in cut]
    passed = call(passed_body, out(count, width), ids, keys, w0, w1, w2, w4, w3, w5, near, mid, far,
                  flops=2 * count * width * depth)
    rows = call(rows_body, out(replicas * half, depth), ids, *mine, *rest[:-1])
    size = half // PARTS
    weight_grad = call(last_body, out(replicas * half, depth), ids, rest[-1], rows,
                       blocks={1: pl.BlockSpec(memory_space=pl.ANY)}, aliases={2: 0},
                       place=pl.BlockSpec((size, depth), lambda i, ids: ((1 - ids[8]) * PARTS + PARTS - 1, 0)))
    return weight_grad[None], passed.reshape(normed.shape)


def solution(mesh):
    in_specs = (
        P("section", None, ("shard", "replica"), None),
        P("section", None, ("shard", "replica"), None),
        P(None, ("shard", "replica")),
        P("section", "shard", None),
    )
    out_specs = (P("section", "shard", None), P("section", None, ("shard", "replica"), None))

    def body(normed, key_cotangent, positions, key_weight):
        pairs = (
            mesh.shape["shard"] == 4
            and mesh.shape["replica"] == 2
            and key_weight.shape[1] * 4 == normed.shape[3]
            and key_weight.shape[1] % 1024 == 0
        )
        form = pair_device if pairs else general_device
        return form(normed, key_cotangent, positions, key_weight)

    return jax.shard_map(body, mesh=mesh, in_specs=in_specs, out_specs=out_specs, check_vma=False)
```
